32 devices in a mesh: grp: 4 (over y, x), span: 8 (over z, core).
Axes of the slice: x: 2, y: 2, z: 4, core: 2. Of those that a mesh axis runs over, the one named last changes fastest.
Arguments:
- traces: bfloat16 [1024, 61440], P('grp', 'span'), may hold values from -1200 to 1200
- seg_starts: int32 [16], replicated, may hold values from 0 to 57344, as said below
- pair_offsets: int32 [1024, 32], P(('grp', 'span')), may hold values from 1 to 64, as said below
Outputs:
- correlations: bfloat16 [1024, 32, 512], P(('grp', 'span'))
The draws below stay inside these ranges and needn't reach their ends.
Inputs may be any that keep to these rules, and one draw needn't show every extreme that they name: `seg_starts`: segments may intersect; one starts at 0 and one at 57344. `pair_offsets`: each channel lists 32 different offsets; its partner is the channel plus the offset.
All inputs are finite; a program needn't handle non-finite values.
Results may differ from the reference program's by a relative error of at most 0.015.
Values may be sent and summed in bfloat16 or wider, within the bound.
A program may use at most 128 MiB of HBM per device.

```python
import math
import jax
import jax.numpy as jnp
from jax import lax

CH_GRP = 256
L = 4096
BINS = 1024
BIN0 = 64
HALF = 32
LAGS = 512
MAXOFF = 64
NPART = 32
SEGS = 16
SAMPLES = 61440
CHANNELS = 1024
N_GRP = 4


def draw_traces(key, part):
    key_noise = jax.random.fold_in(key, 11)
    key_gain = jax.random.fold_in(key, 12)
    key_colour = jax.random.fold_in(key, 13)
    key_envelope = jax.random.fold_in(key, 15)
    white_noise = jnp.clip(jax.random.normal(key_noise, (CHANNELS, SAMPLES + 1), jnp.float32), -4.0, 4.0)
    channel_gain = jnp.exp(jax.random.uniform(key_gain, (CHANNELS, 1), jnp.float32, 0.0, math.log(10.0)))
    colour = jax.random.uniform(key_colour, (CHANNELS, 1), jnp.float32, -0.9, 0.9)
    block_count = (SAMPLES + 127) // 128
    envelope = jnp.exp(jax.random.uniform(key_envelope, (1, block_count), jnp.float32, 0.0, math.log(10.0)))
    envelope = jnp.repeat(envelope, 128, axis=1)[:, :SAMPLES]
    values = channel_gain * envelope * (white_noise[:, 1:] + colour * white_noise[:, :-1])
    return values.astype(jnp.bfloat16)


def draw_seg_starts(key, part):
    starts_drawn = jax.random.randint(jax.random.fold_in(key, 3), (SEGS,), 0, SAMPLES - L + 1, dtype=jnp.int32)
    return starts_drawn.at[0].set(0).at[1].set(SAMPLES - L)


def draw_pair_offsets(key, part):
    scores = jax.random.randint(jax.random.fold_in(key, 5), (CHANNELS, MAXOFF), 0, 1 << 20, dtype=jnp.int32) * 128
    scores = scores + jnp.arange(MAXOFF, dtype=jnp.int32)[None, :]
    scores = scores.at[0, 0].set(-2).at[0, MAXOFF - 1].set(-1)
    ranking = jnp.argsort(scores, axis=1)[:, :NPART]
    return (ranking + 1).astype(jnp.int32)


def setup_inputs(seed: int = 0) -> dict:
    keys = jax.random.split(jax.random.key(seed), 4)
    traces = draw_traces(jax.random.fold_in(keys[3], 71), 0)
    seg_starts = draw_seg_starts(jax.random.fold_in(keys[3], 71), 0)
    pair_offsets = draw_pair_offsets(jax.random.fold_in(keys[3], 71), 0)
    return dict(traces=traces, seg_starts=seg_starts, pair_offsets=pair_offsets)


def taper_window():
    sample_index = jnp.arange(L, dtype=jnp.float32)
    return 0.5 - 0.5 * jnp.cos(2.0 * math.pi / L * (sample_index + 0.5))

def whiten(real_part, imag_part):
    power_sum = real_part * real_part + imag_part * imag_part
    smooth = lax.reduce_window(power_sum, jnp.array(0.0, power_sum.dtype), lax.add, (1, 1, 2 * HALF + 1), (1, 1, 1), 'VALID') / (2 * HALF + 1)
    inverse = lax.rsqrt(smooth + 1e-06)
    band_real = real_part[..., HALF:HALF + BINS] * inverse
    band_imag = imag_part[..., HALF:HALF + BINS] * inverse
    return jnp.stack([band_real, band_imag], axis=1).astype(jnp.bfloat16)

def group_spectra(channel_rows, seg_starts):
    segments = jax.vmap(lambda seg_start: lax.dynamic_slice_in_dim(channel_rows, seg_start, L, 1), out_axes=1)(seg_starts)
    tapered = segments.astype(jnp.float32) * taper_window()
    transform = jnp.fft.rfft(tapered, axis=-1)[..., BIN0 - HALF:BIN0 + BINS + HALF]
    return whiten(jnp.real(transform).astype(jnp.float32), jnp.imag(transform).astype(jnp.float32))

def cross_spectra(own_rows, extended, offsets):
    row_total = own_rows.shape[0]
    block_rows = 16 if row_total % 16 == 0 else row_total
    halo_rows = extended.shape[0] - row_total

    def one_block(block_index):
        first_row = block_index * block_rows
        own_block = lax.dynamic_slice_in_dim(own_rows, first_row, block_rows, 0).astype(jnp.float32)
        others = lax.dynamic_slice_in_dim(extended, first_row, block_rows + halo_rows, 0).astype(jnp.float32)
        wanted = lax.dynamic_slice_in_dim(offsets, first_row, block_rows, 0)
        partner_index = (wanted + jnp.arange(block_rows, dtype=jnp.int32)[:, None]).astype(jnp.int32)
        rotated = jnp.stack([own_block[:, 1], -own_block[:, 0]], axis=1)
        gram_real = jnp.einsum('icsf,jcsf->ijf', own_block, others)
        gram_imag = jnp.einsum('icsf,jcsf->ijf', rotated, others)
        cross_real = jnp.take_along_axis(gram_real, partner_index[:, :, None], axis=1)
        cross_imag = jnp.take_along_axis(gram_imag, partner_index[:, :, None], axis=1)
        return jnp.stack([cross_real, cross_imag], axis=2)
    result = lax.map(one_block, jnp.arange(row_total // block_rows, dtype=jnp.int32))
    return result.reshape((row_total,) + result.shape[2:])

def lag_table():
    bin_index = jnp.arange(BINS, dtype=jnp.int32) + BIN0
    lag_index = jnp.arange(LAGS, dtype=jnp.int32) - LAGS // 2
    phase = jnp.mod(bin_index[:, None] * lag_index[None, :], L)
    angles = phase.astype(jnp.float32) * (2.0 * math.pi / L)
    return jnp.concatenate([jnp.cos(angles), -jnp.sin(angles)], axis=0).astype(jnp.bfloat16)

def reference(traces, seg_starts, pair_offsets):
    grouped = traces.reshape(N_GRP, CH_GRP, SAMPLES)
    spectra = lax.map(lambda channel_rows: group_spectra(channel_rows, seg_starts), grouped)
    spectra = spectra.reshape((CHANNELS,) + spectra.shape[2:])
    extended = jnp.concatenate([spectra, jnp.zeros((MAXOFF,) + spectra.shape[1:], jnp.bfloat16)], axis=0)
    cross_spec = cross_spectra(spectra, extended, pair_offsets).astype(jnp.bfloat16)
    flat_rows = cross_spec.reshape(CHANNELS * NPART, 2 * BINS)
    lag_scale = 1.0 / math.sqrt(SEGS * BINS)
    correlated = jnp.dot(flat_rows, lag_table(), preferred_element_type=jnp.float32) * lag_scale
    return correlated.reshape(CHANNELS, NPART, LAGS).astype(jnp.bfloat16)
```

```python
import functools
import math

import jax
import jax.numpy as jnp
import ml_dtypes
import numpy as np
from jax import lax
from jax.experimental import pallas as pl
from jax.experimental.pallas import tpu as pltpu
from jax.sharding import PartitionSpec as P

L = 4096
BINS = 1024
BIN0 = 64
HALF = 32
LAGS = 512
MAXOFF = 64

LANES = 128
SPLIT = L // LANES
PAIRED = SPLIT // 2
FOLD = BINS // LANES
TILE = 2 * FOLD
BAND = BINS + LANES
SIDE = L // 2
TOGETHER = 16
UNROLLED = 8
STEP_CHANNELS = 8


def times(value, turn):
    re, im = value
    angle = 2.0 * math.pi * turn
    c, s = math.cos(angle), math.sin(angle)
    if abs(s) < 1e-12:
        return (re, im) if c > 0 else (-re, -im)
    if abs(abs(c) - abs(s)) < 1e-12:
        r = abs(c)
        if c > 0 and s < 0:
            return (re + im) * r, (im - re) * r
        if c < 0 and s < 0:
            return (im - re) * r, (re + im) * -r
    if abs(c) < 1e-12 and s < 0:
        return im, -re
    return re * c - im * s, re * s + im * c


def complex_dft(values):
    n = len(values)
    if n == 1:
        return values
    half = n // 2
    low, high = values[:half], values[half:]
    even = [(a[0] + b[0], a[1] + b[1]) for a, b in zip(low, high)]
    odd = [(a[0] - b[0], a[1] - b[1]) for a, b in zip(low, high)]
    odd = [times(v, -i / n) for i, v in enumerate(odd)]
    result = [None] * n
    result[0::2] = complex_dft(even)
    result[1::2] = complex_dft(odd)
    return result


def real_dft(values):
    n = len(values)
    if n == 2:
        return {0: (values[0] + values[1], None), 1: (values[0] - values[1], None)}
    half, quarter = n // 2, n // 4
    result = {2 * r: y for r, y in real_dft([values[i] + values[i + half] for i in range(half)]).items()}
    odd = []
    for i in range(quarter):
        re = values[i] - values[i + half]
        im = values[i + quarter + half] - values[i + quarter]
        odd.append(times((re, im), -i / n))
    for m, y in enumerate(complex_dft(odd)):
        result[4 * m + 1] = y
    return result


@functools.cache
def residues():
    present = real_dft([np.zeros(1)] * SPLIT)
    return [0] + sorted(r for r in present if r not in (0, SPLIT // 2))


@functools.cache
def lane_bins():
    rows = []
    for p, r in enumerate(residues()):
        for kind in (r, SPLIT - r if p else SPLIT // 2):
            rows.append(kind + SPLIT * np.arange(2, 2 + BINS // SPLIT))
    return np.concatenate(rows)


@functools.cache
def side_bins():
    rows = []
    for p, r in enumerate(residues()):
        kinds = (r, SPLIT - r if p else SPLIT // 2)
        rows.append(np.array([k + SPLIT * q for k in kinds for q in (1, 2 + BINS // SPLIT)]))
    return rows


def transform_columns(p, bins):
    r = residues()[p]
    n = np.arange(LANES)
    angles = (n[:, None] * bins[None, :] % L) * (2.0 * np.pi / L)
    cos, sin = np.cos(angles), np.sin(angles)
    table = np.zeros((2, LANES, 2, len(bins)))
    if p == 0:
        first = bins % SPLIT == 0
        for source, use in ((0, first), (1, ~first)):
            table[source, :, 0] = cos * use
            table[source, :, 1] = -sin * use
    else:
        sign = np.where(bins % SPLIT == r, 1.0, -1.0)
        table[0, :, 0] = cos
        table[1, :, 0] = sin * sign
        table[0, :, 1] = -sin
        table[1, :, 1] = cos * sign
    return table.reshape(2 * LANES, 2, len(bins))


def high_low(table):
    table = table.astype(np.float32)
    high = table.astype(ml_dtypes.bfloat16)
    low = (table - high.astype(np.float32)).astype(ml_dtypes.bfloat16)
    return high, low


@functools.cache
def forward_tables():
    band = lane_bins().reshape(PAIRED, LANES // 2)
    highs, lows = [], []
    for p in range(PAIRED):
        columns = transform_columns(p, band[p])
        if p % 2:
            columns = columns[:, ::-1]
        high, low = high_low(columns.reshape(2 * LANES, LANES))
        side = np.zeros((2 * LANES, LANES))
        width = LANES // PAIRED
        side[:, p * width : (p + 1) * width] = transform_columns(p, side_bins()[p]).reshape(2 * LANES, width)
        side_high, side_low = high_low(side)
        high = np.concatenate([high, side_high], axis=1)
        low = np.concatenate([low, side_low], axis=1)
        highs.append(high)
        lows.append(low)
    return np.stack(highs), np.stack(lows)


@functools.cache
def band_table():
    side = np.concatenate([np.concatenate([b, b]) for b in side_bins()])
    rows = np.concatenate([lane_bins(), side])
    near = np.abs(rows[:, None] - lane_bins()[None, :]) <= HALF
    return near.astype(np.float32).astype(ml_dtypes.bfloat16)


@functools.cache
def lag_table():
    lags = np.arange(LAGS) - LAGS // 2
    angles = (lane_bins()[:, None] * lags[None, :] % L) * (2.0 * np.pi / L)
    table = np.stack([np.cos(angles), -np.sin(angles)]).reshape(2, FOLD, LANES, LAGS)
    table = table.transpose(1, 0, 2, 3).reshape(FOLD, 2 * LANES, LAGS)
    return table.astype(np.float32).astype(ml_dtypes.bfloat16)


@functools.cache
def taper_table():
    n = (np.arange(L)[None, :] - np.arange(LANES)[:, None]) % L
    taper = 0.5 - 0.5 * np.cos(2.0 * np.pi / L * (n + 0.5))
    return taper.astype(np.float32).reshape(LANES, SPLIT, LANES)


def slot_kernel(partners, scale, info_ref, place_ref, offsets_ref, own_ref, sib_ref, halo_ref, sib_halo_ref,
                next_ref, sib_next_ref, next_halo_ref, sib_next_halo_ref,
                taper_ref, high_ref, low_ref, band_ref, lag_ref, out_ref,
                win_ref, y_ref, spec_ref, power_ref, side_ref, ext_ref, real_ref, imag_ref, sems):
    count = info_ref[0]
    rows = win_ref.shape[0]
    channels, per = own_ref.shape
    here = rows - MAXOFF
    length = rows * TILE

    def transfers(act):
        for parity in (0, 1):
            first = ((own_ref, halo_ref), (next_ref, next_halo_ref))
            second = ((sib_ref, sib_halo_ref), (sib_next_ref, sib_next_halo_ref))
            if parity:
                first, second = second, first
            for j in range(rows // here):
                row = place_ref[0] + j * here
                for beyond in (0, 1):
                    inside = row >= channels if beyond else row < channels

                    @pl.when((info_ref[1] == parity) & inside)
                    def _(first=first, second=second, j=j, row=row, beyond=beyond):
                        source = pl.ds(pl.multiple_of(row - beyond * channels, 16), here)
                        target = pl.ds(j * here, here)
                        for side, (main, halo) in enumerate((first[beyond], second[beyond])):
                            lanes = pl.ds(SIDE + side * per, per)
                            act(pltpu.make_async_copy(
                                main.at[source, :], win_ref.at[target, lanes], sems.at[4 * j + 2 * side]))
                            lanes = pl.ds(side * (2 * per + SIDE), SIDE)
                            act(pltpu.make_async_copy(
                                halo.at[source, :], win_ref.at[target, lanes], sems.at[4 * j + 2 * side + 1]))

    transfers(lambda c: c.start())
    transfers(lambda c: c.wait())

    lane = lax.broadcasted_iota(jnp.int32, (8, LANES), 1)
    wide = lax.broadcasted_iota(jnp.int32, (2 * rows, LANES), 1)

    def two_segments(m, carry):
        def transform(s):
            position = info_ref[2 + 2 * m + s]
            block = position // LANES
            within = lax.rem(position, LANES)

            def transform_rows(i, carry):
                row = pl.ds(pl.multiple_of(i * 16, 16), 16)
                for half in (0, 1):
                    def piece(j):
                        at = pl.ds(pl.multiple_of((block + j) * LANES, LANES), LANES)
                        return win_ref[row, at].astype(jnp.float32)[8 * half : 8 * half + 8]
                    values = []
                    for j in range(SPLIT):
                        value = piece(j)
                        if j == 0:
                            value = jnp.where(lane < within, piece(SPLIT), value)
                        values.append(value * taper_ref[within, j : j + 1, :])
                    parts = real_dft(values)
                    at = pl.ds(pl.multiple_of(s * rows + i * 16 + 8 * half, 8), 8)
                    for p, r in enumerate(residues()):
                        re, im = parts[r]
                        if p == 0:
                            im = parts[SPLIT // 2][0]
                        y_ref[p, at, :LANES] = re
                        y_ref[p, at, LANES:] = im
                return carry

            lax.fori_loop(0, rows // 16, transform_rows, 0)

        transform(0)
        transform(1)
        side_ref[...] = jnp.zeros_like(side_ref)

        def two(g, carry):
            bands = []
            side = side_ref[...]
            for odd in (0, 1):
                p = 2 * g + odd
                y = y_ref[p]
                high = y.astype(jnp.bfloat16)
                low = (y - high.astype(jnp.float32)).astype(jnp.bfloat16)
                both = jnp.concatenate([high, low], axis=0)
                made = jnp.dot(both, high_ref[p], preferred_element_type=jnp.float32)
                made = made[: 2 * rows] + made[2 * rows :]
                made += jnp.dot(high, low_ref[p], preferred_element_type=jnp.float32)
                bands.append(made[:, :LANES])
                side += made[:, LANES:]
            side_ref[...] = side
            left = wide < LANES // 2
            re = jnp.where(left, bands[0], bands[1])
            im = pltpu.roll(jnp.where(left, bands[1], bands[0]), LANES // 2, 1)
            spec_ref[0, g] = re
            spec_ref[1, g] = im
            power_ref[g] = (re * re + im * im).astype(jnp.bfloat16)
            return carry

        lax.fori_loop(0, FOLD, two, 0, unroll=2)
        side = side_ref[...]
        power_ref[FOLD] = (side * side).astype(jnp.bfloat16)

        power = jnp.concatenate([power_ref[g] for g in range(FOLD + 1)], axis=1)
        for g in range(FOLD):
            if g % 2 == 0:
                total = jnp.dot(power, band_ref[:, g * LANES : (g + 2) * LANES], preferred_element_type=jnp.float32)
                inverse = lax.rsqrt(total * (1.0 / (2 * HALF + 1)) + 1e-06)
            factor = inverse[:, g % 2 * LANES : (g % 2 + 1) * LANES]
            for part in (0, 1):
                whitened = spec_ref[part, g] * factor
                for s in (0, 1):
                    first = pl.multiple_of((2 * m + s) * length, length) + (part * FOLD + g)
                    ext_ref[pl.ds(first, rows, stride=TILE), :] = whitened[s * rows : (s + 1) * rows]
        return carry

    lax.fori_loop(0, (count + 1) // 2, two_segments, 0)

    def tile(s, channel):
        at = pl.multiple_of((s * rows + channel) * TILE, TILE)
        return ext_ref[pl.ds(at, FOLD), :], ext_ref[pl.ds(at + FOLD, FOLD), :]

    def some_pairs(chunk, fixed, n, carry):
        local = n // (partners // TOGETHER)
        k0 = lax.rem(n, partners // TOGETHER) * TOGETHER
        own = chunk * STEP_CHANNELS + local
        others = [own + offsets_ref[own, k0 + u] for u in range(TOGETHER)]

        def one(s, sums):
            ar, ai = tile(s, own)
            result = []
            for u in range(TOGETHER):
                br, bi = tile(s, others[u])
                result.append(sums[2 * u] + (ar * br + ai * bi))
                result.append(sums[2 * u + 1] + (ai * br - ar * bi))
            return tuple(result)

        sums = (jnp.zeros((FOLD, LANES), jnp.float32),) * (2 * TOGETHER)
        if fixed is None:
            sums = lax.fori_loop(0, count, one, sums)
        else:
            for s in range(fixed):
                sums = one(s, sums)
        for u in range(TOGETHER):
            at = pl.ds(pl.multiple_of((n * TOGETHER + u) * FOLD, FOLD), FOLD)
            real_ref[at, :] = sums[2 * u]
            imag_ref[at, :] = sums[2 * u + 1]
        return carry

    pairs = STEP_CHANNELS * partners

    def one_chunk(chunk, carry):
        for fixed in range(1, UNROLLED + 1):
            @pl.when(count == fixed)
            def _(fixed=fixed):
                lax.fori_loop(0, pairs // TOGETHER, functools.partial(some_pairs, chunk, fixed), 0)

        @pl.when((count == 0) | (count > UNROLLED))
        def _():
            lax.fori_loop(0, pairs // TOGETHER, functools.partial(some_pairs, chunk, None), 0)

        result = jnp.zeros((pairs, LAGS), jnp.float32)
        for g in range(FOLD):
            real = real_ref[pl.ds(g, pairs, stride=FOLD), :]
            imag = imag_ref[pl.ds(g, pairs, stride=FOLD), :]
            both = jnp.concatenate([real, imag], axis=1).astype(jnp.bfloat16)
            result += jnp.dot(both, lag_ref[g], preferred_element_type=jnp.float32)
        out_ref[pl.ds(pl.multiple_of(chunk * pairs, pairs), pairs), :] = (result * scale).astype(jnp.bfloat16)
        return carry

    lax.fori_loop(0, here // STEP_CHANNELS, one_chunk, 0)


def one_slot(info, place, offsets, pieces):
    here, partners = offsets.shape
    segs = info.shape[0] - 2
    channels, per = pieces[0].shape
    rows = here + MAXOFF
    slots = segs + segs % 2
    pairs = STEP_CHANNELS * partners
    high, low = forward_tables()
    tables = [taper_table(), high, low, band_table(), lag_table()]
    return pl.pallas_call(
        functools.partial(slot_kernel, partners, 1.0 / math.sqrt(segs * BINS)),
        in_specs=[pl.BlockSpec(memory_space=pltpu.SMEM)] * 3
        + [pl.BlockSpec(memory_space=pl.ANY)] * len(pieces)
        + [pl.BlockSpec(memory_space=pltpu.VMEM)] * len(tables),
        out_specs=pl.BlockSpec(memory_space=pltpu.VMEM),
        out_shape=jax.ShapeDtypeStruct((here * partners, LAGS), jnp.bfloat16),
        scratch_shapes=[
            pltpu.VMEM((rows, 2 * per + 2 * SIDE), jnp.bfloat16),
            pltpu.VMEM((PAIRED, 2 * rows, 2 * LANES), jnp.float32),
            pltpu.VMEM((2, FOLD, 2 * rows, LANES), jnp.float32),
            pltpu.VMEM((FOLD + 1, 2 * rows, LANES), jnp.bfloat16),
            pltpu.VMEM((2 * rows, LANES), jnp.float32),
            pltpu.VMEM((slots * rows * TILE, LANES), jnp.float32),
            pltpu.VMEM((pairs * FOLD, LANES), jnp.float32),
            pltpu.VMEM((pairs * FOLD, LANES), jnp.float32),
            pltpu.SemaphoreType.DMA((4 * (rows // here),)),
        ],
        compiler_params=pltpu.CompilerParams(vmem_limit_bytes=44 * 2**20),
        cost_estimate=pl.CostEstimate(flops=15 * 10**9, transcendentals=0, bytes_accessed=20 * 2**20),
    )(info, place, offsets, *pieces, *[jnp.asarray(t) for t in tables])


def orders(chips):
    table = []
    for z in range(chips // 2):
        table.append(list(range(z)) + list(range(chips - 1, z, -1)) + [z])
    return table + [[chips - 1 - d for d in row] for row in reversed(table)]


def on_device(traces, seg_starts, pair_offsets):
    span, groups = lax.axis_size("span"), lax.axis_size("grp")
    chips = span // 2
    here = pair_offsets.shape[0]
    channels, per = traces.shape
    segs = seg_starts.shape[0]
    me = lax.axis_index("span")
    z, core = me // 2, lax.rem(me, 2)

    beside = [(i, i - 1 if i % 2 == 0 else i + 1) for i in range(1, span - 1)]
    swap = [(i, i ^ 1) for i in range(span)]
    back = [(g * span + i, (g - 1) * span + i) for g in range(1, groups) for i in range(span)]
    sibling = lambda x: lax.ppermute(x, "span", swap)

    edge = jnp.where(core == 0, traces[:, :SIDE], traces[:, per - SIDE :])
    after = lax.ppermute(traces[:MAXOFF], ("grp", "span"), back)
    halo = lax.ppermute(edge, "span", beside)
    sib = sibling(traces)
    sib_halo = sibling(halo)
    after_halo = lax.ppermute(halo[:MAXOFF], ("grp", "span"), back)
    sib_after = sibling(after)
    sib_after_halo = sibling(after_halo)
    pieces = [traces, sib, halo, sib_halo, after, sib_after, after_halo, sib_after_halo]

    offsets = pair_offsets
    bit = 1
    while bit < span:
        other = lax.ppermute(offsets, "span", [(i, i ^ bit) for i in range(span)])
        upper = (me & bit) != 0
        low, high = jnp.where(upper, other, offsets), jnp.where(upper, offsets, other)
        offsets = jnp.concatenate([low, high], axis=0)
        bit *= 2

    chip_of = (seg_starts + SIDE) // (2 * per)
    mine = chip_of == z
    index = jnp.arange(segs, dtype=jnp.int32)
    rank = jnp.sum(mine[None, :] & (index[None, :] < index[:, None]), axis=1, dtype=jnp.int32)
    at = seg_starts - (z * 2 * per - SIDE)
    slot = jnp.arange(segs, dtype=jnp.int32)[:, None]
    listed = jnp.sum(jnp.where(mine[None, :] & (rank[None, :] == slot), at[None, :], 0), axis=1)
    info = jnp.concatenate([jnp.sum(mine.astype(jnp.int32))[None], core[None], listed]).astype(jnp.int32)

    order = jnp.asarray(np.array(orders(chips), np.int32))[z]
    slots = [None]
    for k in range(chips):
        first = (2 * order[k] + core) * here
        wanted = lax.dynamic_slice_in_dim(offsets, first, here, 0)
        slots.append(one_slot(info, first[None], wanted, pieces))

    def own_part(t, upward):
        place = z if upward else chips - 1 - z
        value = slots[t]
        for other in range(chips // 2, chips - 1):
            if 0 < t - other:
                value = jnp.where(place == other, slots[t - other], value)
        return value

    arrived = {}
    for t in range(1, chips):
        for upward in (True, False):
            value = own_part(t, upward)
            if upward in arrived:
                value = (value.astype(jnp.float32) + arrived[upward].astype(jnp.float32)).astype(jnp.bfloat16)
            route = []
            for place in range(t):
                for c in (0, 1):
                    a, b = (place, place + 1) if upward else (chips - 1 - place, chips - 2 - place)
                    route.append((2 * a + c, 2 * b + c))
            arrived[upward] = lax.ppermute(value, "span", route)
    total = slots[chips].astype(jnp.float32)
    total += arrived[True].astype(jnp.float32) + arrived[False].astype(jnp.float32)
    return total.astype(jnp.bfloat16).reshape(here, pair_offsets.shape[1], LAGS)


def solution(mesh):
    placed = (P("grp", "span"), P(), P(("grp", "span"), None))
    return jax.shard_map(
        on_device,
        mesh=mesh,
        in_specs=placed,
        out_specs=P(("grp", "span"), None, None),
        check_vma=False,
    )
```

```python
import functools
import math

import jax
import jax.numpy as jnp
import ml_dtypes
import numpy as np
from jax import lax
from jax.experimental import pallas as pl
from jax.experimental.pallas import tpu as pltpu
from jax.sharding import PartitionSpec as P

L = 4096
BINS = 1024
BIN0 = 64
HALF = 32
LAGS = 512
MAXOFF = 64

LANES = 128
SPLIT = L // LANES
PAIRED = SPLIT // 2
FOLD = BINS // LANES
TILE = 2 * FOLD
BAND = BINS + LANES
SIDE = L // 2
TOGETHER = 16
UNROLLED = 8
STEP_CHANNELS = 8


def times(value, turn):
    re, im = value
    angle = 2.0 * math.pi * turn
    c, s = math.cos(angle), math.sin(angle)
    if abs(s) < 1e-12:
        return (re, im) if c > 0 else (-re, -im)
    if abs(abs(c) - abs(s)) < 1e-12:
        r = abs(c)
        if c > 0 and s < 0:
            return (re + im) * r, (im - re) * r
        if c < 0 and s < 0:
            return (im - re) * r, (re + im) * -r
    if abs(c) < 1e-12 and s < 0:
        return im, -re
    return re * c - im * s, re * s + im * c


def complex_dft(values):
    n = len(values)
    if n == 1:
        return values
    half = n // 2
    low, high = values[:half], values[half:]
    even = [(a[0] + b[0], a[1] + b[1]) for a, b in zip(low, high)]
    odd = [(a[0] - b[0], a[1] - b[1]) for a, b in zip(low, high)]
    odd = [times(v, -i / n) for i, v in enumerate(odd)]
    result = [None] * n
    result[0::2] = complex_dft(even)
    result[1::2] = complex_dft(odd)
    return result


def real_dft(values):
    n = len(values)
    if n == 2:
        return {0: (values[0] + values[1], None), 1: (values[0] - values[1], None)}
    half, quarter = n // 2, n // 4
    result = {2 * r: y for r, y in real_dft([values[i] + values[i + half] for i in range(half)]).items()}
    odd = []
    for i in range(quarter):
        re = values[i] - values[i + half]
        im = values[i + quarter + half] - values[i + quarter]
        odd.append(times((re, im), -i / n))
    for m, y in enumerate(complex_dft(odd)):
        result[4 * m + 1] = y
    return result


@functools.cache
def residues():
    present = real_dft([np.zeros(1)] * SPLIT)
    return [0] + sorted(r for r in present if r not in (0, SPLIT // 2))


@functools.cache
def lane_bins():
    rows = []
    for p, r in enumerate(residues()):
        for kind in (r, SPLIT - r if p else SPLIT // 2):
            rows.append(kind + SPLIT * np.arange(2, 2 + BINS // SPLIT))
    return np.concatenate(rows)


@functools.cache
def side_bins():
    rows = []
    for p, r in enumerate(residues()):
        kinds = (r, SPLIT - r if p else SPLIT // 2)
        rows.append(np.array([k + SPLIT * q for k in kinds for q in (1, 2 + BINS // SPLIT)]))
    return rows


def transform_columns(p, bins):
    r = residues()[p]
    n = np.arange(LANES)
    angles = (n[:, None] * bins[None, :] % L) * (2.0 * np.pi / L)
    cos, sin = np.cos(angles), np.sin(angles)
    table = np.zeros((2, LANES, 2, len(bins)))
    if p == 0:
        first = bins % SPLIT == 0
        for source, use in ((0, first), (1, ~first)):
            table[source, :, 0] = cos * use
            table[source, :, 1] = -sin * use
    else:
        sign = np.where(bins % SPLIT == r, 1.0, -1.0)
        table[0, :, 0] = cos
        table[1, :, 0] = sin * sign
        table[0, :, 1] = -sin
        table[1, :, 1] = cos * sign
    return table.reshape(2 * LANES, 2, len(bins))


def high_low(table):
    table = table.astype(np.float32)
    high = table.astype(ml_dtypes.bfloat16)
    low = (table - high.astype(np.float32)).astype(ml_dtypes.bfloat16)
    return high, low


@functools.cache
def forward_tables():
    band = lane_bins().reshape(PAIRED, LANES // 2)
    highs, lows = [], []
    for p in range(PAIRED):
        columns = transform_columns(p, band[p])
        if p % 2:
            columns = columns[:, ::-1]
        high, low = high_low(columns.reshape(2 * LANES, LANES))
        side = np.zeros((2 * LANES, LANES))
        width = LANES // PAIRED
        side[:, p * width : (p + 1) * width] = transform_columns(p, side_bins()[p]).reshape(2 * LANES, width)
        side_high, side_low = high_low(side)
        high = np.concatenate([high, side_high], axis=1)
        low = np.concatenate([low, side_low], axis=1)
        highs.append(high)
        lows.append(low)
    return np.stack(highs), np.stack(lows)


@functools.cache
def band_table():
    side = np.concatenate([np.concatenate([b, b]) for b in side_bins()])
    rows = np.concatenate([lane_bins(), side])
    near = np.abs(rows[:, None] - lane_bins()[None, :]) <= HALF
    return near.astype(np.float32).astype(ml_dtypes.bfloat16)


@functools.cache
def lag_table():
    lags = np.arange(LAGS) - LAGS // 2
    angles = (lane_bins()[:, None] * lags[None, :] % L) * (2.0 * np.pi / L)
    table = np.stack([np.cos(angles), -np.sin(angles)]).reshape(2, FOLD, LANES, LAGS)
    table = table.transpose(1, 0, 2, 3).reshape(FOLD, 2 * LANES, LAGS)
    return table.astype(np.float32).astype(ml_dtypes.bfloat16)


@functools.cache
def taper_table():
    n = (np.arange(L)[None, :] - np.arange(LANES)[:, None]) % L
    taper = 0.5 - 0.5 * np.cos(2.0 * np.pi / L * (n + 0.5))
    return taper.astype(np.float32).reshape(LANES, SPLIT, LANES)


def slot_kernel(partners, scale, info_ref, place_ref, offsets_ref, own_ref, sib_ref, halo_ref, sib_halo_ref,
                next_ref, sib_next_ref, next_halo_ref, sib_next_halo_ref,
                taper_ref, high_ref, low_ref, band_ref, lag_ref, out_ref,
                win_ref, y_ref, spec_ref, power_ref, side_ref, ext_ref, real_ref, imag_ref, sems):
    count = info_ref[0]
    rows = win_ref.shape[0]
    channels, per = own_ref.shape
    here = rows - MAXOFF
    length = rows * TILE

    def transfers(act):
        for parity in (0, 1):
            first = ((own_ref, halo_ref), (next_ref, next_halo_ref))
            second = ((sib_ref, sib_halo_ref), (sib_next_ref, sib_next_halo_ref))
            if parity:
                first, second = second, first
            for j in range(rows // here):
                row = place_ref[0] + j * here
                for beyond in (0, 1):
                    inside = row >= channels if beyond else row < channels

                    @pl.when((info_ref[1] == parity) & inside)
                    def _(first=first, second=second, j=j, row=row, beyond=beyond):
                        source = pl.ds(pl.multiple_of(row - beyond * channels, 16), here)
                        target = pl.ds(j * here, here)
                        for side, (main, halo) in enumerate((first[beyond], second[beyond])):
                            lanes = pl.ds(SIDE + side * per, per)
                            act(pltpu.make_async_copy(
                                main.at[source, :], win_ref.at[target, lanes], sems.at[4 * j + 2 * side]))
                            lanes = pl.ds(side * (2 * per + SIDE), SIDE)
                            act(pltpu.make_async_copy(
                                halo.at[source, :], win_ref.at[target, lanes], sems.at[4 * j + 2 * side + 1]))

    transfers(lambda c: c.start())
    transfers(lambda c: c.wait())

    lane = lax.broadcasted_iota(jnp.int32, (8, LANES), 1)
    wide = lax.broadcasted_iota(jnp.int32, (2 * rows, LANES), 1)

    def two_segments(m, carry):
        def transform(s):
            position = info_ref[2 + 2 * m + s]
            block = position // LANES
            within = lax.rem(position, LANES)

            def transform_rows(i, carry):
                row = pl.ds(pl.multiple_of(i * 16, 16), 16)
                for half in (0, 1):
                    def piece(j):
                        at = pl.ds(pl.multiple_of((block + j) * LANES, LANES), LANES)
                        return win_ref[row, at].astype(jnp.float32)[8 * half : 8 * half + 8]
                    values = []
                    for j in range(SPLIT):
                        value = piece(j)
                        if j == 0:
                            value = jnp.where(lane < within, piece(SPLIT), value)
                        values.append(value * taper_ref[within, j : j + 1, :])
                    parts = real_dft(values)
                    at = pl.ds(pl.multiple_of(s * rows + i * 16 + 8 * half, 8), 8)
                    for p, r in enumerate(residues()):
                        re, im = parts[r]
                        if p == 0:
                            im = parts[SPLIT // 2][0]
                        y_ref[p, at, :LANES] = re
                        y_ref[p, at, LANES:] = im
                return carry

            lax.fori_loop(0, rows // 16, transform_rows, 0)

        transform(0)
        transform(1)
        side_ref[...] = jnp.zeros_like(side_ref)

        def two(g, carry):
            bands = []
            side = side_ref[...]
            for odd in (0, 1):
                p = 2 * g + odd
                y = y_ref[p]
                high = y.astype(jnp.bfloat16)
                low = (y - high.astype(jnp.float32)).astype(jnp.bfloat16)
                both = jnp.concatenate([high, low], axis=0)
                made = jnp.dot(both, high_ref[p], preferred_element_type=jnp.float32)
                made = made[: 2 * rows] + made[2 * rows :]
                made += jnp.dot(high, low_ref[p], preferred_element_type=jnp.float32)
                bands.append(made[:, :LANES])
                side += made[:, LANES:]
            side_ref[...] = side
            left = wide < LANES // 2
            re = jnp.where(left, bands[0], bands[1])
            im = pltpu.roll(jnp.where(left, bands[1], bands[0]), LANES // 2, 1)
            spec_ref[0, g] = re
            spec_ref[1, g] = im
            power_ref[g] = (re * re + im * im).astype(jnp.bfloat16)
            return carry

        lax.fori_loop(0, FOLD, two, 0, unroll=8)
        side = side_ref[...]
        power_ref[FOLD] = (side * side).astype(jnp.bfloat16)

        power = jnp.concatenate([power_ref[g] for g in range(FOLD + 1)], axis=1)
        for g in range(FOLD):
            if g % 2 == 0:
                total = jnp.dot(power, band_ref[:, g * LANES : (g + 2) * LANES], preferred_element_type=jnp.float32)
                inverse = lax.rsqrt(total * (1.0 / (2 * HALF + 1)) + 1e-06)
            factor = inverse[:, g % 2 * LANES : (g % 2 + 1) * LANES]
            for part in (0, 1):
                whitened = spec_ref[part, g] * factor
                for s in (0, 1):
                    first = pl.multiple_of((2 * m + s) * length, length) + (part * FOLD + g)
                    ext_ref[pl.ds(first, rows, stride=TILE), :] = whitened[s * rows : (s + 1) * rows]
        return carry

    lax.fori_loop(0, (count + 1) // 2, two_segments, 0)

    def tile(s, channel):
        at = pl.multiple_of((s * rows + channel) * TILE, TILE)
        return ext_ref[pl.ds(at, FOLD), :], ext_ref[pl.ds(at + FOLD, FOLD), :]

    def some_pairs(chunk, fixed, n, carry):
        local = n // (partners // TOGETHER)
        k0 = lax.rem(n, partners // TOGETHER) * TOGETHER
        own = chunk * STEP_CHANNELS + local
        others = [own + offsets_ref[own, k0 + u] for u in range(TOGETHER)]

        def one(s, sums):
            ar, ai = tile(s, own)
            result = []
            for u in range(TOGETHER):
                br, bi = tile(s, others[u])
                result.append(sums[2 * u] + (ar * br + ai * bi))
                result.append(sums[2 * u + 1] + (ai * br - ar * bi))
            return tuple(result)

        sums = (jnp.zeros((FOLD, LANES), jnp.float32),) * (2 * TOGETHER)
        if fixed is None:
            sums = lax.fori_loop(0, count, one, sums)
        else:
            for s in range(fixed):
                sums = one(s, sums)
        for u in range(TOGETHER):
            at = pl.ds(pl.multiple_of((n * TOGETHER + u) * FOLD, FOLD), FOLD)
            real_ref[at, :] = sums[2 * u]
            imag_ref[at, :] = sums[2 * u + 1]
        return carry

    pairs = STEP_CHANNELS * partners

    def one_chunk(chunk, carry):
        for fixed in range(1, UNROLLED + 1):
            @pl.when(count == fixed)
            def _(fixed=fixed):
                lax.fori_loop(0, pairs // TOGETHER, functools.partial(some_pairs, chunk, fixed), 0)

        @pl.when((count == 0) | (count > UNROLLED))
        def _():
            lax.fori_loop(0, pairs // TOGETHER, functools.partial(some_pairs, chunk, None), 0)

        result = jnp.zeros((pairs, LAGS), jnp.float32)
        for g in range(FOLD):
            real = real_ref[pl.ds(g, pairs, stride=FOLD), :]
            imag = imag_ref[pl.ds(g, pairs, stride=FOLD), :]
            both = jnp.concatenate([real, imag], axis=1).astype(jnp.bfloat16)
            result += jnp.dot(both, lag_ref[g], preferred_element_type=jnp.float32)
        out_ref[pl.ds(pl.multiple_of(chunk * pairs, pairs), pairs), :] = (result * scale).astype(jnp.bfloat16)
        return carry

    lax.fori_loop(0, here // STEP_CHANNELS, one_chunk, 0)


def gather_kernel(span, x_ref, out_ref, send_sems, recv_sems, own_sem):
    group, me = lax.axis_index("grp"), lax.axis_index("span")
    peers = [(group, lax.rem(me + d, span)) for d in range(1, span)]
    barrier = pltpu.get_barrier_semaphore()
    for peer in peers:
        pl.semaphore_signal(barrier, inc=1, device_id=peer, device_id_type=pl.DeviceIdType.MESH)
    own = pltpu.make_async_copy(x_ref, out_ref.at[me], own_sem)
    own.start()
    pl.semaphore_wait(barrier, span - 1)
    copies = [
        pltpu.make_async_remote_copy(
            src_ref=x_ref, dst_ref=out_ref.at[me], send_sem=send_sems.at[d], recv_sem=recv_sems.at[d],
            device_id=peer, device_id_type=pl.DeviceIdType.MESH,
        )
        for d, peer in enumerate(peers)
    ]
    for c in copies:
        c.start()
    own.wait()
    for c in copies:
        c.wait()


def gathered(x, span):
    return pl.pallas_call(
        functools.partial(gather_kernel, span),
        in_specs=[pl.BlockSpec(memory_space=pltpu.VMEM)],
        out_specs=pl.BlockSpec(memory_space=pltpu.VMEM),
        out_shape=jax.ShapeDtypeStruct((span, *x.shape), x.dtype),
        scratch_shapes=[
            pltpu.SemaphoreType.DMA((span - 1,)),
            pltpu.SemaphoreType.DMA((span - 1,)),
            pltpu.SemaphoreType.DMA,
        ],
        compiler_params=pltpu.CompilerParams(collective_id=0, has_side_effects=True),
    )(x)


def listing_kernel(starts_ref, place_ref, traces_ref, info_ref, head_ref, edge_ref, edge_head_ref, sems):
    channels, per = traces_ref.shape

    def transfers(act):
        act(pltpu.make_async_copy(traces_ref.at[pl.ds(0, MAXOFF), :], head_ref, sems.at[0]))
        for core in (0, 1):
            @pl.when(place_ref[1] == core)
            def _(core=core):
                lanes = pl.ds(core * (per - SIDE), SIDE)
                act(pltpu.make_async_copy(traces_ref.at[:, lanes], edge_ref, sems.at[1]))
                act(pltpu.make_async_copy(traces_ref.at[pl.ds(0, MAXOFF), lanes], edge_head_ref, sems.at[2]))

    transfers(lambda c: c.start())
    for i in range(info_ref.shape[0]):
        info_ref[i] = 0
    count = jnp.int32(0)
    for s in range(starts_ref.shape[0]):
        start = starts_ref[s]
        mine = (start + SIDE) // (2 * per) == place_ref[0]

        @pl.when(mine)
        def _(start=start, count=count):
            info_ref[2 + count] = start - (place_ref[0] * 2 * per - SIDE)

        count = count + mine.astype(jnp.int32)
    info_ref[0] = count
    info_ref[1] = place_ref[1]
    transfers(lambda c: c.wait())


def listing(starts, place, traces):
    channels, per = traces.shape
    shapes = [(MAXOFF, per), (channels, SIDE), (MAXOFF, SIDE)]
    return pl.pallas_call(
        listing_kernel,
        in_specs=[pl.BlockSpec(memory_space=pltpu.SMEM)] * 2 + [pl.BlockSpec(memory_space=pl.ANY)],
        out_specs=[pl.BlockSpec(memory_space=pltpu.SMEM)] + [pl.BlockSpec(memory_space=pltpu.VMEM)] * 3,
        out_shape=[jax.ShapeDtypeStruct((2 + starts.shape[0],), jnp.int32)]
        + [jax.ShapeDtypeStruct(shape, traces.dtype) for shape in shapes],
        scratch_shapes=[pltpu.SemaphoreType.DMA((3,))],
        compiler_params=pltpu.CompilerParams(vmem_limit_bytes=24 * 2**20),
    )(starts, place, traces)


def one_slot(info, place, offsets, pieces, tables):
    here, partners = offsets.shape
    segs = info.shape[0] - 2
    channels, per = pieces[0].shape
    rows = here + MAXOFF
    slots = segs + segs % 2
    pairs = STEP_CHANNELS * partners
    return pl.pallas_call(
        functools.partial(slot_kernel, partners, 1.0 / math.sqrt(segs * BINS)),
        in_specs=[pl.BlockSpec(memory_space=pltpu.SMEM)] * 3
        + [pl.BlockSpec(memory_space=pl.ANY)] * len(pieces)
        + [pl.BlockSpec(memory_space=pltpu.VMEM)] * len(tables),
        out_specs=pl.BlockSpec(memory_space=pltpu.VMEM),
        out_shape=jax.ShapeDtypeStruct((here * partners, LAGS), jnp.bfloat16),
        scratch_shapes=[
            pltpu.VMEM((rows, 2 * per + 2 * SIDE), jnp.bfloat16),
            pltpu.VMEM((PAIRED, 2 * rows, 2 * LANES), jnp.float32),
            pltpu.VMEM((2, FOLD, 2 * rows, LANES), jnp.float32),
            pltpu.VMEM((FOLD + 1, 2 * rows, LANES), jnp.bfloat16),
            pltpu.VMEM((2 * rows, LANES), jnp.float32),
            pltpu.VMEM((slots * rows * TILE, LANES), jnp.float32),
            pltpu.VMEM((pairs * FOLD, LANES), jnp.float32),
            pltpu.VMEM((pairs * FOLD, LANES), jnp.float32),
            pltpu.SemaphoreType.DMA((4 * (rows // here),)),
        ],
        compiler_params=pltpu.CompilerParams(vmem_limit_bytes=40 * 2**20),
        cost_estimate=pl.CostEstimate(flops=15 * 10**9, transcendentals=0, bytes_accessed=20 * 2**20),
    )(info, place, offsets, *pieces, *tables)


def orders(chips):
    table = []
    for z in range(chips // 2):
        table.append(list(range(z)) + list(range(chips - 1, z, -1)) + [z])
    return table + [[chips - 1 - d for d in row] for row in reversed(table)]


def on_device(traces, seg_starts, pair_offsets):
    span, groups = lax.axis_size("span"), lax.axis_size("grp")
    chips = span // 2
    here = pair_offsets.shape[0]
    channels, per = traces.shape
    segs = seg_starts.shape[0]
    me = lax.axis_index("span")
    z, core = me // 2, lax.rem(me, 2)

    beside = [(i, i - 1 if i % 2 == 0 else i + 1) for i in range(1, span - 1)]
    swap = [(i, i ^ 1) for i in range(span)]
    back = [(g * span + i, (g - 1) * span + i) for g in range(1, groups) for i in range(span)]
    sibling = lambda x: lax.ppermute(x, "span", swap)

    high, low = forward_tables()
    tables = [jnp.asarray(t) for t in (taper_table(), high, low, band_table(), lag_table())]
    info, head, edge, edge_head = listing(seg_starts, jnp.stack([z, core]).astype(jnp.int32), traces)
    across = [((g + 1) * span + i, g * span + j) for g in range(groups - 1) for i, j in beside]
    halo = lax.ppermute(edge, "span", beside)
    after = lax.ppermute(head, ("grp", "span"), back)
    after_halo = lax.ppermute(edge_head, ("grp", "span"), across)
    sib = sibling(traces)
    edge, listed = lax.optimization_barrier((edge, pair_offsets))
    offsets = gathered(listed, span).reshape(channels, -1)
    halo, after_halo, offsets = lax.optimization_barrier((halo, after_halo, offsets))
    sib_halo = sibling(halo)
    sib_after = sibling(after)
    sib_after_halo = sibling(after_halo)
    pieces = [traces, sib, halo, sib_halo, after, sib_after, after_halo, sib_after_halo]

    order = jnp.asarray(np.array(orders(chips), np.int32))[z]
    slots = [None]
    for k in range(chips):
        first = (2 * order[k] + core) * here
        wanted = lax.dynamic_slice_in_dim(offsets, first, here, 0)
        slots.append(one_slot(info, first[None], wanted, pieces, tables))

    def own_part(t, upward):
        place = z if upward else chips - 1 - z
        value = slots[t]
        for other in range(chips // 2, chips - 1):
            if 0 < t - other:
                value = jnp.where(place == other, slots[t - other], value)
        return value

    arrived = {}
    for t in range(1, chips):
        for upward in (True, False):
            value = own_part(t, upward)
            if upward in arrived:
                value = (value.astype(jnp.float32) + arrived[upward].astype(jnp.float32)).astype(jnp.bfloat16)
            route = []
            for place in range(t):
                for c in (0, 1):
                    a, b = (place, place + 1) if upward else (chips - 1 - place, chips - 2 - place)
                    route.append((2 * a + c, 2 * b + c))
            arrived[upward] = lax.ppermute(value, "span", route)
    total = slots[chips].astype(jnp.float32)
    total += arrived[True].astype(jnp.float32) + arrived[False].astype(jnp.float32)
    return total.astype(jnp.bfloat16).reshape(here, pair_offsets.shape[1], LAGS)


def solution(mesh):
    placed = (P("grp", "span"), P(), P(("grp", "span"), None))
    return jax.shard_map(
        on_device,
        mesh=mesh,
        in_specs=placed,
        out_specs=P(("grp", "span"), None, None),
        check_vma=False,
    )
```

```python
import functools
import math

import jax
import jax.numpy as jnp
import ml_dtypes
import numpy as np
from jax import lax
from jax.experimental import pallas as pl
from jax.experimental.pallas import tpu as pltpu
from jax.sharding import PartitionSpec as P

L = 4096
BINS = 1024
BIN0 = 64
HALF = 32
LAGS = 512
MAXOFF = 64

LANES = 128
SPLIT = L // LANES
PAIRED = SPLIT // 2
FOLD = BINS // LANES
TILE = 2 * FOLD
BAND = BINS + LANES
SIDE = L // 2
TOGETHER = 16
UNROLLED = 8
STEP_CHANNELS = 8


def times(value, turn):
    re, im = value
    angle = 2.0 * math.pi * turn
    c, s = math.cos(angle), math.sin(angle)
    if abs(s) < 1e-12:
        return (re, im) if c > 0 else (-re, -im)
    if abs(abs(c) - abs(s)) < 1e-12:
        r = abs(c)
        if c > 0 and s < 0:
            return (re + im) * r, (im - re) * r
        if c < 0 and s < 0:
            return (im - re) * r, (re + im) * -r
    if abs(c) < 1e-12 and s < 0:
        return im, -re
    return re * c - im * s, re * s + im * c


def complex_dft(values):
    n = len(values)
    if n == 1:
        return values
    half = n // 2
    low, high = values[:half], values[half:]
    even = [(a[0] + b[0], a[1] + b[1]) for a, b in zip(low, high)]
    odd = [(a[0] - b[0], a[1] - b[1]) for a, b in zip(low, high)]
    odd = [times(v, -i / n) for i, v in enumerate(odd)]
    result = [None] * n
    result[0::2] = complex_dft(even)
    result[1::2] = complex_dft(odd)
    return result


def real_dft(values):
    n = len(values)
    if n == 2:
        return {0: (values[0] + values[1], None), 1: (values[0] - values[1], None)}
    half, quarter = n // 2, n // 4
    result = {2 * r: y for r, y in real_dft([values[i] + values[i + half] for i in range(half)]).items()}
    odd = []
    for i in range(quarter):
        re = values[i] - values[i + half]
        im = values[i + quarter + half] - values[i + quarter]
        odd.append(times((re, im), -i / n))
    for m, y in enumerate(complex_dft(odd)):
        result[4 * m + 1] = y
    return result


@functools.cache
def residues():
    present = real_dft([np.zeros(1)] * SPLIT)
    return [0] + sorted(r for r in present if r not in (0, SPLIT // 2))


@functools.cache
def lane_bins():
    rows = []
    for p, r in enumerate(residues()):
        for kind in (r, SPLIT - r if p else SPLIT // 2):
            rows.append(kind + SPLIT * np.arange(2, 2 + BINS // SPLIT))
    return np.concatenate(rows)


@functools.cache
def side_bins():
    rows = []
    for p, r in enumerate(residues()):
        kinds = (r, SPLIT - r if p else SPLIT // 2)
        rows.append(np.array([k + SPLIT * q for k in kinds for q in (1, 2 + BINS // SPLIT)]))
    return rows


def transform_columns(p, bins):
    r = residues()[p]
    n = np.arange(LANES)
    angles = (n[:, None] * bins[None, :] % L) * (2.0 * np.pi / L)
    cos, sin = np.cos(angles), np.sin(angles)
    table = np.zeros((2, LANES, 2, len(bins)))
    if p == 0:
        first = bins % SPLIT == 0
        for source, use in ((0, first), (1, ~first)):
            table[source, :, 0] = cos * use
            table[source, :, 1] = -sin * use
    else:
        sign = np.where(bins % SPLIT == r, 1.0, -1.0)
        table[0, :, 0] = cos
        table[1, :, 0] = sin * sign
        table[0, :, 1] = -sin
        table[1, :, 1] = cos * sign
    return table.reshape(2 * LANES, 2, len(bins))


def high_low(table):
    table = table.astype(np.float32)
    high = table.astype(ml_dtypes.bfloat16)
    low = (table - high.astype(np.float32)).astype(ml_dtypes.bfloat16)
    return high, low


@functools.cache
def forward_tables():
    band = lane_bins().reshape(PAIRED, LANES // 2)
    highs, lows = [], []
    for p in range(PAIRED):
        columns = transform_columns(p, band[p])
        if p % 2:
            columns = columns[:, ::-1]
        high, low = high_low(columns.reshape(2 * LANES, LANES))
        side = np.zeros((2 * LANES, LANES))
        width = LANES // PAIRED
        side[:, p * width : (p + 1) * width] = transform_columns(p, side_bins()[p]).reshape(2 * LANES, width)
        side_high, side_low = high_low(side)
        high = np.concatenate([high, side_high], axis=1)
        low = np.concatenate([low, side_low], axis=1)
        highs.append(high)
        lows.append(low)
    return np.stack(highs), np.stack(lows)


@functools.cache
def band_table():
    side = np.concatenate([np.concatenate([b, b]) for b in side_bins()])
    rows = np.concatenate([lane_bins(), side])
    near = np.abs(rows[:, None] - lane_bins()[None, :]) <= HALF
    return near.astype(np.float32).astype(ml_dtypes.bfloat16)


@functools.cache
def lag_table():
    lags = np.arange(LAGS) - LAGS // 2
    angles = (lane_bins()[:, None] * lags[None, :] % L) * (2.0 * np.pi / L)
    table = np.stack([np.cos(angles), -np.sin(angles)]).reshape(2, FOLD, LANES, LAGS)
    table = table.transpose(1, 0, 2, 3).reshape(FOLD, 2 * LANES, LAGS)
    return table.astype(np.float32).astype(ml_dtypes.bfloat16)


@functools.cache
def taper_table():
    n = (np.arange(L)[None, :] - np.arange(LANES)[:, None]) % L
    taper = 0.5 - 0.5 * np.cos(2.0 * np.pi / L * (n + 0.5))
    return taper.astype(np.float32).reshape(LANES, SPLIT, LANES)


def slot_kernel(partners, scale, info_ref, place_ref, offsets_ref, own_ref, sib_ref, halo_ref, sib_halo_ref,
                next_ref, sib_next_ref, next_halo_ref, sib_next_halo_ref,
                taper_ref, high_ref, low_ref, band_all, lag_all, out_ref,
                band_ref, lag_ref, win_ref, y_ref, spec_ref, power_ref, side_ref, ext_ref, real_ref, imag_ref, sems, late_sems):
    count = info_ref[0]
    rows = win_ref.shape[0]
    channels, per = own_ref.shape
    here = rows - MAXOFF
    length = rows * TILE

    def transfers(act):
        for parity in (0, 1):
            first = ((own_ref, halo_ref), (next_ref, next_halo_ref))
            second = ((sib_ref, sib_halo_ref), (sib_next_ref, sib_next_halo_ref))
            if parity:
                first, second = second, first
            for j in range(rows // here):
                row = place_ref[0] + j * here
                for beyond in (0, 1):
                    inside = row >= channels if beyond else row < channels

                    @pl.when((info_ref[1] == parity) & inside)
                    def _(first=first, second=second, j=j, row=row, beyond=beyond):
                        source = pl.ds(pl.multiple_of(row - beyond * channels, 16), here)
                        target = pl.ds(j * here, here)
                        for side, (main, halo) in enumerate((first[beyond], second[beyond])):
                            lanes = pl.ds(SIDE + side * per, per)
                            act(pltpu.make_async_copy(
                                main.at[source, :], win_ref.at[target, lanes], sems.at[4 * j + 2 * side]))
                            lanes = pl.ds(side * (2 * per + SIDE), SIDE)
                            act(pltpu.make_async_copy(
                                halo.at[source, :], win_ref.at[target, lanes], sems.at[4 * j + 2 * side + 1]))

    band_load = pltpu.make_async_copy(band_all, band_ref, late_sems.at[0])
    lag_load = pltpu.make_async_copy(lag_all, lag_ref, late_sems.at[1])
    transfers(lambda c: c.start())
    band_load.start()
    transfers(lambda c: c.wait())
    lag_load.start()

    lane = lax.broadcasted_iota(jnp.int32, (8, LANES), 1)
    wide = lax.broadcasted_iota(jnp.int32, (2 * rows, LANES), 1)

    def two_segments(m, carry):
        def transform(s):
            position = info_ref[2 + 2 * m + s]
            block = position // LANES
            within = lax.rem(position, LANES)

            def transform_rows(i, carry):
                row = pl.ds(pl.multiple_of(i * 16, 16), 16)
                for half in (0, 1):
                    def piece(j):
                        at = pl.ds(pl.multiple_of((block + j) * LANES, LANES), LANES)
                        return win_ref[row, at].astype(jnp.float32)[8 * half : 8 * half + 8]
                    values = []
                    for j in range(SPLIT):
                        value = piece(j)
                        if j == 0:
                            value = jnp.where(lane < within, piece(SPLIT), value)
                        values.append(value * taper_ref[within, j : j + 1, :])
                    parts = real_dft(values)
                    at = pl.ds(pl.multiple_of(s * rows + i * 16 + 8 * half, 8), 8)
                    for p, r in enumerate(residues()):
                        re, im = parts[r]
                        if p == 0:
                            im = parts[SPLIT // 2][0]
                        y_ref[p, at, :LANES] = re
                        y_ref[p, at, LANES:] = im
                return carry

            lax.fori_loop(0, rows // 16, transform_rows, 0)

        transform(0)
        transform(1)
        side_ref[...] = jnp.zeros_like(side_ref)

        def two(g, carry):
            bands = []
            side = side_ref[...]
            for odd in (0, 1):
                p = 2 * g + odd
                y = y_ref[p]
                high = y.astype(jnp.bfloat16)
                low = (y - high.astype(jnp.float32)).astype(jnp.bfloat16)
                both = jnp.concatenate([high, low], axis=0)
                made = jnp.dot(both, high_ref[p], preferred_element_type=jnp.float32)
                made = made[: 2 * rows] + made[2 * rows :]
                made += jnp.dot(high, low_ref[p], preferred_element_type=jnp.float32)
                bands.append(made[:, :LANES])
                side += made[:, LANES:]
            side_ref[...] = side
            left = wide < LANES // 2
            re = jnp.where(left, bands[0], bands[1])
            im = pltpu.roll(jnp.where(left, bands[1], bands[0]), LANES // 2, 1)
            spec_ref[0, g] = re
            spec_ref[1, g] = im
            power_ref[g] = (re * re + im * im).astype(jnp.bfloat16)
            return carry

        lax.fori_loop(0, FOLD, two, 0, unroll=8)
        @pl.when(m == 0)
        def _():
            band_load.wait()

        side = side_ref[...]
        power_ref[FOLD] = (side * side).astype(jnp.bfloat16)

        power = jnp.concatenate([power_ref[g] for g in range(FOLD + 1)], axis=1)
        for g in range(FOLD):
            if g % 2 == 0:
                total = jnp.dot(power, band_ref[:, g * LANES : (g + 2) * LANES], preferred_element_type=jnp.float32)
                inverse = lax.rsqrt(total * (1.0 / (2 * HALF + 1)) + 1e-06)
            factor = inverse[:, g % 2 * LANES : (g % 2 + 1) * LANES]
            for part in (0, 1):
                whitened = spec_ref[part, g] * factor
                for s in (0, 1):
                    first = pl.multiple_of((2 * m + s) * length, length) + (part * FOLD + g)
                    ext_ref[pl.ds(first, rows, stride=TILE), :] = whitened[s * rows : (s + 1) * rows]
        return carry

    lax.fori_loop(0, (count + 1) // 2, two_segments, 0)

    @pl.when(count == 0)
    def _():
        band_load.wait()

    lag_load.wait()

    def tile(s, channel):
        at = pl.multiple_of((s * rows + channel) * TILE, TILE)
        return ext_ref[pl.ds(at, FOLD), :], ext_ref[pl.ds(at + FOLD, FOLD), :]

    def some_pairs(chunk, fixed, n, carry):
        local = n // (partners // TOGETHER)
        k0 = lax.rem(n, partners // TOGETHER) * TOGETHER
        own = chunk * STEP_CHANNELS + local
        others = [own + offsets_ref[own, k0 + u] for u in range(TOGETHER)]

        def one(s, sums):
            ar, ai = tile(s, own)
            result = []
            for u in range(TOGETHER):
                br, bi = tile(s, others[u])
                result.append(sums[2 * u] + (ar * br + ai * bi))
                result.append(sums[2 * u + 1] + (ai * br - ar * bi))
            return tuple(result)

        sums = (jnp.zeros((FOLD, LANES), jnp.float32),) * (2 * TOGETHER)
        if fixed is None:
            sums = lax.fori_loop(0, count, one, sums)
        else:
            for s in range(fixed):
                sums = one(s, sums)
        for u in range(TOGETHER):
            at = pl.ds(pl.multiple_of((n * TOGETHER + u) * FOLD, FOLD), FOLD)
            real_ref[at, :] = sums[2 * u]
            imag_ref[at, :] = sums[2 * u + 1]
        return carry

    pairs = STEP_CHANNELS * partners

    def one_chunk(chunk, carry):
        for fixed in range(1, UNROLLED + 1):
            @pl.when(count == fixed)
            def _(fixed=fixed):
                lax.fori_loop(0, pairs // TOGETHER, functools.partial(some_pairs, chunk, fixed), 0)

        @pl.when((count == 0) | (count > UNROLLED))
        def _():
            lax.fori_loop(0, pairs // TOGETHER, functools.partial(some_pairs, chunk, None), 0)

        result = jnp.zeros((pairs, LAGS), jnp.float32)
        for g in range(FOLD):
            real = real_ref[pl.ds(g, pairs, stride=FOLD), :]
            imag = imag_ref[pl.ds(g, pairs, stride=FOLD), :]
            both = jnp.concatenate([real, imag], axis=1).astype(jnp.bfloat16)
            result += jnp.dot(both, lag_ref[g], preferred_element_type=jnp.float32)
        out_ref[pl.ds(pl.multiple_of(chunk * pairs, pairs), pairs), :] = (result * scale).astype(jnp.bfloat16)
        return carry

    lax.fori_loop(0, here // STEP_CHANNELS, one_chunk, 0)


def gather_kernel(span, x_ref, out_ref, send_sems, recv_sems, own_sem):
    group, me = lax.axis_index("grp"), lax.axis_index("span")
    peers = [(group, lax.rem(me + d, span)) for d in range(1, span)]
    barrier = pltpu.get_barrier_semaphore()
    for peer in peers:
        pl.semaphore_signal(barrier, inc=1, device_id=peer, device_id_type=pl.DeviceIdType.MESH)
    own = pltpu.make_async_copy(x_ref, out_ref.at[me], own_sem)
    own.start()
    pl.semaphore_wait(barrier, span - 1)
    copies = [
        pltpu.make_async_remote_copy(
            src_ref=x_ref, dst_ref=out_ref.at[me], send_sem=send_sems.at[d], recv_sem=recv_sems.at[d],
            device_id=peer, device_id_type=pl.DeviceIdType.MESH,
        )
        for d, peer in enumerate(peers)
    ]
    for c in copies:
        c.start()
    own.wait()
    for c in copies:
        c.wait()


def gathered(x, span):
    return pl.pallas_call(
        functools.partial(gather_kernel, span),
        in_specs=[pl.BlockSpec(memory_space=pltpu.VMEM)],
        out_specs=pl.BlockSpec(memory_space=pltpu.VMEM),
        out_shape=jax.ShapeDtypeStruct((span, *x.shape), x.dtype),
        scratch_shapes=[
            pltpu.SemaphoreType.DMA((span - 1,)),
            pltpu.SemaphoreType.DMA((span - 1,)),
            pltpu.SemaphoreType.DMA,
        ],
        compiler_params=pltpu.CompilerParams(collective_id=0, has_side_effects=True),
    )(x)


def listing_kernel(starts_ref, place_ref, traces_ref, info_ref, head_ref, edge_ref, edge_head_ref, sems):
    channels, per = traces_ref.shape

    def transfers(act):
        act(pltpu.make_async_copy(traces_ref.at[pl.ds(0, MAXOFF), :], head_ref, sems.at[0]))
        for core in (0, 1):
            @pl.when(place_ref[1] == core)
            def _(core=core):
                lanes = pl.ds(core * (per - SIDE), SIDE)
                act(pltpu.make_async_copy(traces_ref.at[:, lanes], edge_ref, sems.at[1]))
                act(pltpu.make_async_copy(traces_ref.at[pl.ds(0, MAXOFF), lanes], edge_head_ref, sems.at[2]))

    transfers(lambda c: c.start())
    for i in range(info_ref.shape[0]):
        info_ref[i] = 0
    count = jnp.int32(0)
    for s in range(starts_ref.shape[0]):
        start = starts_ref[s]
        mine = (start + SIDE) // (2 * per) == place_ref[0]

        @pl.when(mine)
        def _(start=start, count=count):
            info_ref[2 + count] = start - (place_ref[0] * 2 * per - SIDE)

        count = count + mine.astype(jnp.int32)
    info_ref[0] = count
    info_ref[1] = place_ref[1]
    transfers(lambda c: c.wait())


def listing(starts, place, traces):
    channels, per = traces.shape
    shapes = [(MAXOFF, per), (channels, SIDE), (MAXOFF, SIDE)]
    return pl.pallas_call(
        listing_kernel,
        in_specs=[pl.BlockSpec(memory_space=pltpu.SMEM)] * 2 + [pl.BlockSpec(memory_space=pl.ANY)],
        out_specs=[pl.BlockSpec(memory_space=pltpu.SMEM)] + [pl.BlockSpec(memory_space=pltpu.VMEM)] * 3,
        out_shape=[jax.ShapeDtypeStruct((2 + starts.shape[0],), jnp.int32)]
        + [jax.ShapeDtypeStruct(shape, traces.dtype) for shape in shapes],
        scratch_shapes=[pltpu.SemaphoreType.DMA((3,))],
        compiler_params=pltpu.CompilerParams(vmem_limit_bytes=60 * 2**20),
    )(starts, place, traces)


def one_slot(info, place, offsets, pieces, tables):
    here, partners = offsets.shape
    segs = info.shape[0] - 2
    channels, per = pieces[0].shape
    rows = here + MAXOFF
    slots = segs + segs % 2
    pairs = STEP_CHANNELS * partners
    return pl.pallas_call(
        functools.partial(slot_kernel, partners, 1.0 / math.sqrt(segs * BINS)),
        in_specs=[pl.BlockSpec(memory_space=pltpu.SMEM)] * 3
        + [pl.BlockSpec(memory_space=pl.ANY)] * len(pieces)
        + [pl.BlockSpec(memory_space=pltpu.VMEM)] * 3
        + [pl.BlockSpec(memory_space=pl.ANY)] * 2,
        out_specs=pl.BlockSpec(memory_space=pltpu.VMEM),
        out_shape=jax.ShapeDtypeStruct((here * partners, LAGS), jnp.bfloat16),
        scratch_shapes=[pltpu.VMEM(t.shape, t.dtype) for t in tables[3:]]
        + [
            pltpu.VMEM((rows, 2 * per + 2 * SIDE), jnp.bfloat16),
            pltpu.VMEM((PAIRED, 2 * rows, 2 * LANES), jnp.float32),
            pltpu.VMEM((2, FOLD, 2 * rows, LANES), jnp.float32),
            pltpu.VMEM((FOLD + 1, 2 * rows, LANES), jnp.bfloat16),
            pltpu.VMEM((2 * rows, LANES), jnp.float32),
            pltpu.VMEM((slots * rows * TILE, LANES), jnp.float32),
            pltpu.VMEM((pairs * FOLD, LANES), jnp.float32),
            pltpu.VMEM((pairs * FOLD, LANES), jnp.float32),
            pltpu.SemaphoreType.DMA((4 * (rows // here),)),
            pltpu.SemaphoreType.DMA((2,)),
        ],
        compiler_params=pltpu.CompilerParams(vmem_limit_bytes=42 * 2**20),
        cost_estimate=pl.CostEstimate(flops=15 * 10**9, transcendentals=0, bytes_accessed=20 * 2**20),
    )(info, place, offsets, *pieces, *tables)


def orders(chips):
    table = []
    for z in range(chips // 2):
        table.append(list(range(z)) + list(range(chips - 1, z, -1)) + [z])
    return table + [[chips - 1 - d for d in row] for row in reversed(table)]


def on_device(traces, seg_starts, pair_offsets):
    span, groups = lax.axis_size("span"), lax.axis_size("grp")
    chips = span // 2
    here = pair_offsets.shape[0]
    channels, per = traces.shape
    segs = seg_starts.shape[0]
    me = lax.axis_index("span")
    z, core = me // 2, lax.rem(me, 2)

    beside = [(i, i - 1 if i % 2 == 0 else i + 1) for i in range(1, span - 1)]
    swap = [(i, i ^ 1) for i in range(span)]
    back = [(g * span + i, (g - 1) * span + i) for g in range(1, groups) for i in range(span)]
    sibling = lambda x: lax.ppermute(x, "span", swap)

    high, low = forward_tables()
    tables = [jnp.asarray(t) for t in (taper_table(), high, low, band_table(), lag_table())]
    info, head, edge, edge_head = listing(seg_starts, jnp.stack([z, core]).astype(jnp.int32), traces)
    across = [((g + 1) * span + i, g * span + j) for g in range(groups - 1) for i, j in beside]
    halo = lax.ppermute(edge, "span", beside)
    after = lax.ppermute(head, ("grp", "span"), back)
    after_halo = lax.ppermute(edge_head, ("grp", "span"), across)
    sib = sibling(traces)
    edge, listed = lax.optimization_barrier((edge, pair_offsets))
    offsets = gathered(listed, span).reshape(channels, -1)
    halo, after_halo, offsets = lax.optimization_barrier((halo, after_halo, offsets))
    sib_halo = sibling(halo)
    sib_after = sibling(after)
    sib_after_halo = sibling(after_halo)
    pieces = [traces, sib, halo, sib_halo, after, sib_after, after_halo, sib_after_halo]

    order = jnp.asarray(np.array(orders(chips), np.int32))[z]
    slots = [None]
    for k in range(chips):
        first = (2 * order[k] + core) * here
        wanted = lax.dynamic_slice_in_dim(offsets, first, here, 0)
        slots.append(one_slot(info, first[None], wanted, pieces, tables))

    def own_part(t, upward):
        place = z if upward else chips - 1 - z
        value = slots[t]
        for other in range(chips // 2, chips - 1):
            if 0 < t - other:
                value = jnp.where(place == other, slots[t - other], value)
        return value

    arrived = {}
    for t in range(1, chips):
        for upward in (True, False):
            value = own_part(t, upward)
            if upward in arrived:
                value = (value.astype(jnp.float32) + arrived[upward].astype(jnp.float32)).astype(jnp.bfloat16)
            route = []
            for place in range(t):
                for c in (0, 1):
                    a, b = (place, place + 1) if upward else (chips - 1 - place, chips - 2 - place)
                    route.append((2 * a + c, 2 * b + c))
            arrived[upward] = lax.ppermute(value, "span", route)
    total = slots[chips].astype(jnp.float32)
    total += arrived[True].astype(jnp.float32) + arrived[False].astype(jnp.float32)
    return total.astype(jnp.bfloat16).reshape(here, pair_offsets.shape[1], LAGS)


def solution(mesh):
    placed = (P("grp", "span"), P(), P(("grp", "span"), None))
    return jax.shard_map(
        on_device,
        mesh=mesh,
        in_specs=placed,
        out_specs=P(("grp", "span"), None, None),
        check_vma=False,
    )
```
